128 devices in a mesh: dom: 16 (over y, z), sub: 8 (over x, core).
Axes of the slice: x: 4, y: 4, z: 4, core: 2. Of those that a mesh axis runs over, the one named last changes fastest.
Arguments:
- charges: bfloat16 [65536, 1152], P(('dom', 'sub')), may hold values from -6 to 6
- frac_coords: float32 [3, 65536], P(None, ('dom', 'sub')), may hold values from 0 to 1
- atom_counts: int32 [128], replicated, may hold values from 0 to 512, as said below
- miller: int32 [3, 4096], replicated, may hold values from -10 to 10, as said below
- box: float32 [3], replicated, may hold values from 200 to 400
- cotangent: float32 [128], replicated, may hold values from 0.25 to 4
Outputs:
- grad_charges: float32 [65536, 1152], P(('dom', 'sub'))
- grad_coords: float32 [3, 65536], P(None, ('dom', 'sub'))
The draws below stay inside these ranges and needn't reach their ends.
Inputs may be any that keep to these rules, and one draw needn't show every extreme that they name: `atom_counts`: the counts sum to 32768; some sub-domain holds exactly 512 atoms and some none. `miller`: the k-vectors are distinct and the third index of every k-vector is 1 or more, so no k-vector is zero.
All inputs are finite; a program needn't handle non-finite values.
Results may differ from the reference program's by a relative error of at most 0.005.
Values may be sent and summed in bfloat16 or wider, within the bound.
No kernel may reach another device: no remote copies, remote signals or barrier semaphores. Data moves between devices by JAX's collectives and lax.ppermute only.
A program may use at most 64 MiB of HBM per device.

```python
import math
import jax
import jax.numpy as jnp
from jax import lax

C = 128
MULT = 9
K = 4096
MILLER = 10
RECV = 256
CAP = 512
ATOMS = 32768
ROWS = 65536
DEVICES = 128


def draw_atom_counts(key, part):
    half = DEVICES // 2
    order = jax.random.permutation(jax.random.fold_in(key, 1), DEVICES)
    spread = jax.random.randint(jax.random.fold_in(key, 2), (half,), 0, RECV + 1)
    spread = spread.at[0].set(RECV)
    counts = jnp.zeros((DEVICES,), jnp.int32)
    counts = counts.at[order[:half]].set((RECV + spread).astype(jnp.int32))
    counts = counts.at[order[half:]].set((RECV - spread).astype(jnp.int32))
    return counts


def draw_miller(key, part):
    side = 2 * MILLER + 1
    total = side * side * MILLER
    chosen = jax.random.permutation(jax.random.fold_in(key, 11), total)[:K].astype(jnp.int32)
    height = chosen // (side * side) + 1
    rest = chosen % (side * side)
    first = rest // side - MILLER
    second = rest % side - MILLER
    return jnp.stack([first, second, height], axis=0).astype(jnp.int32)


def level_of(key, shape, shards, least, top_value):
    loudness, own = 1.0, jax.random.fold_in(key, 6)
    for axis_at, blocks in shards:
        steps = jnp.exp(jax.random.uniform(jax.random.fold_in(own, axis_at), (blocks,), jnp.float32, least / len(shards), top_value / len(shards)))
        loudness = loudness * jnp.repeat(steps, shape[axis_at] // blocks).reshape([-1 if axis == axis_at else 1 for axis in range(len(shape))])
    return loudness


def centred(rng, dims, deviation, limit, cuts=(), kind=jnp.bfloat16):
    level = level_of(rng, dims, cuts, -0.22, 0.18) if cuts else 1.0
    entries = jax.random.normal(rng, dims, jnp.float32) * deviation * level
    return jnp.minimum(jnp.maximum(entries, -limit), limit).astype(kind)


def setup_inputs(seed: int = 0) -> dict:
    key_of = jax.random.split(jax.random.key(seed), 7)
    charges = centred(key_of[0], (ROWS, MULT * C), 1.0, 6.0, ((0, 128),))
    frac_coords = jnp.clip(1.0 * jax.random.uniform(key_of[1], (3, ROWS), jnp.float32) ** level_of(key_of[1], (3, ROWS), ((1, 128),), -0.2, 0.2), 0.0, 1.0)
    atom_counts = draw_atom_counts(jax.random.fold_in(key_of[6], 71), 0)
    miller = draw_miller(jax.random.fold_in(key_of[6], 71), 0)
    box = jnp.clip(jnp.exp(jax.random.uniform(key_of[4], (3,), jnp.float32, math.log(200.0), math.log(400.0))), 200.0, 400.0)
    cotangent = jnp.clip(jnp.exp(jax.random.uniform(key_of[5], (C,), jnp.float32, math.log(0.25), math.log(4.0))), 0.25, 4.0)
    return {"charges": charges, "frac_coords": frac_coords, "atom_counts": atom_counts, "miller": miller, "box": box, "cotangent": cotangent}


TWO_PI = 2.0 * math.pi
ROOT_THREE = math.sqrt(3.0)

def unit_tables(miller, box):
    k_vectors = TWO_PI * miller.astype(jnp.float32) / box[:, None]
    k_square = lax.optimization_barrier(jnp.sum(k_vectors * k_vectors, axis=0))
    inverse = 1.0 / jnp.sqrt(k_square)
    unit_x = k_vectors[0] * inverse
    unit_y = k_vectors[1] * inverse
    unit_z = k_vectors[2] * inverse
    zero_row = jnp.zeros_like(unit_x)
    ones_row = jnp.ones_like(unit_x)
    even_table = jnp.stack([ones_row, zero_row, zero_row, zero_row, -ROOT_THREE * unit_x * unit_y, -ROOT_THREE * unit_y * unit_z, -ROOT_THREE * unit_z * unit_x, -0.5 * ROOT_THREE * (unit_x * unit_x - unit_y * unit_y), -0.5 * (3.0 * unit_z * unit_z - 1.0)], axis=0)
    odd_table = jnp.stack([zero_row, unit_x, unit_y, unit_z, zero_row, zero_row, zero_row, zero_row, zero_row], axis=0)
    k_filter = jnp.exp(-0.5 * k_square) / k_square
    return (even_table, odd_table, k_filter)

def split_coords(fraction):
    coarse = fraction.astype(jnp.bfloat16)
    coarse_back = lax.optimization_barrier(coarse).astype(jnp.float32)
    fine_part = (fraction - coarse_back).astype(jnp.bfloat16)
    return jnp.concatenate([coarse, fine_part], axis=0).T

def phase_tiles(coords, k_nums):
    fraction = coords[:, 0:3].astype(jnp.float32) + coords[:, 3:6].astype(jnp.float32)
    numbers = k_nums.astype(jnp.float32)
    angle = TWO_PI * (fraction[:, 0:1] * numbers[0][None, :] + fraction[:, 1:2] * numbers[1][None, :] + fraction[:, 2:3] * numbers[2][None, :])
    return (jnp.cos(angle).astype(jnp.bfloat16), jnp.sin(angle).astype(jnp.bfloat16))

def k_blocks(miller, even_table, odd_table):
    k_count = miller.shape[1]
    k_block = min(k_count, 256)
    block_count = k_count // k_block
    return (miller.reshape(3, block_count, k_block).transpose(1, 0, 2), even_table.reshape(9, block_count, k_block).transpose(1, 0, 2), odd_table.reshape(9, block_count, k_block).transpose(1, 0, 2))

def structure_partial(charges, coords, miller, even_table, odd_table):
    row_width = charges.shape[1]
    channels = row_width // 9
    k_count = miller.shape[1]
    k_block = min(k_count, 256)
    highest = lax.Precision.HIGHEST

    def one_block(inputs):
        k_nums, k_even, k_odd = inputs
        cosine, sine = phase_tiles(coords, k_nums)
        cos_q = jnp.dot(cosine.T, charges, preferred_element_type=jnp.float32).reshape(k_block, 9, channels)
        sin_q = jnp.dot(sine.T, charges, preferred_element_type=jnp.float32).reshape(k_block, 9, channels)
        real_part = jnp.einsum('mk,kmc->kc', k_even, cos_q, precision=highest) - jnp.einsum('mk,kmc->kc', k_odd, sin_q, precision=highest)
        imag_part = jnp.einsum('mk,kmc->kc', k_even, sin_q, precision=highest) + jnp.einsum('mk,kmc->kc', k_odd, cos_q, precision=highest)
        return jnp.stack([real_part, imag_part], axis=1)
    blocks = lax.map(one_block, k_blocks(miller, even_table, odd_table))
    return blocks.reshape(k_count, 2, channels)

def scaled_factors(summed, k_filter, cotangent, atom_total, filter_norm):
    weight = k_filter / (filter_norm * jnp.sqrt(atom_total))
    return (summed * weight[:, None, None] * cotangent[None, None, :]).astype(jnp.bfloat16)

def gradient_rows(charges, coords, miller, even_table, odd_table, factor):
    row_count, row_width = charges.shape
    channels = row_width // 9
    k_count = miller.shape[1]
    k_block = min(k_count, 256)
    block_count = k_count // k_block
    highest = lax.Precision.HIGHEST
    nums_b, even_b, odd_b = k_blocks(miller, even_table, odd_table)
    factor_b = factor.reshape(block_count, k_block, 2, channels)

    def one_block(running, inputs):
        grad_q, grad_f = running
        k_nums, k_even, k_odd, k_factor = inputs
        cosine, sine = phase_tiles(coords, k_nums)
        real_wide = k_factor[:, 0, :].astype(jnp.float32)[:, None, :]
        imag_wide = k_factor[:, 1, :].astype(jnp.float32)[:, None, :]
        even_t = k_even.T[:, :, None]
        odd_t = k_odd.T[:, :, None]
        cos_coef = (even_t * real_wide + odd_t * imag_wide).astype(jnp.bfloat16).reshape(k_block, row_width)
        sin_coef = (even_t * imag_wide - odd_t * real_wide).astype(jnp.bfloat16).reshape(k_block, row_width)
        grad_q = grad_q + jnp.dot(cosine, cos_coef, preferred_element_type=jnp.float32) + jnp.dot(sine, sin_coef, preferred_element_type=jnp.float32)
        with_sin = jnp.dot(charges, sin_coef.T, preferred_element_type=jnp.float32)
        with_cos = jnp.dot(charges, cos_coef.T, preferred_element_type=jnp.float32)
        turning = cosine.astype(jnp.float32) * with_sin - sine.astype(jnp.float32) * with_cos
        grad_f = grad_f + TWO_PI * jnp.dot(turning, k_nums.astype(jnp.float32).T, precision=highest)
        return ((grad_q, grad_f), None)
    start = (jnp.zeros((row_count, row_width), jnp.float32), jnp.zeros((row_count, 3), jnp.float32))
    (grad_q, grad_f), ignored = lax.scan(one_block, start, (nums_b, even_b, odd_b, factor_b))
    return (grad_q, grad_f)

def reference(charges, frac_coords, atom_counts, miller, box, cotangent):
    slot_total = charges.shape[0]
    row_width = charges.shape[1]
    row_index = jnp.arange(slot_total, dtype=jnp.int32)
    is_live = row_index % CAP < atom_counts[row_index // CAP]
    slot_rank = jnp.cumsum(is_live.astype(jnp.int32)) - 1
    target = jnp.where(is_live, slot_rank, ATOMS).astype(jnp.int32)
    picked = jnp.zeros((ATOMS,), jnp.int32).at[target].set(row_index, mode='drop')
    coords = split_coords(frac_coords)
    work_q = charges[picked]
    work_c = coords[picked]
    even_table, odd_table, k_filter = unit_tables(miller, box)
    summed = structure_partial(work_q, work_c, miller, even_table, odd_table)
    filter_norm = jnp.sqrt(jnp.sum(k_filter * k_filter))
    atom_total = jnp.sum(atom_counts).astype(jnp.float32)
    factor = scaled_factors(summed, k_filter, cotangent, atom_total, filter_norm)
    atom_block = math.gcd(ATOMS, 2048)

    def rows_block(inputs):
        block_q, block_c = inputs
        return gradient_rows(block_q, block_c, miller, even_table, odd_table, factor)
    grad_q, grad_f = lax.map(rows_block, (work_q.reshape(-1, atom_block, row_width), work_c.reshape(-1, atom_block, 6)))
    grad_q = grad_q.reshape(ATOMS, row_width)
    grad_f = grad_f.reshape(ATOMS, 3)
    out_q = jnp.zeros((slot_total, row_width), jnp.float32).at[picked].set(grad_q)
    out_f = jnp.zeros((slot_total, 3), jnp.float32).at[picked].set(grad_f)
    return (out_q, out_f.T)
```

```python
import functools
import math

import jax
import jax.numpy as jnp
from jax import lax
from jax.experimental import pallas as pl
from jax.experimental.pallas import tpu as pltpu
from jax.sharding import PartitionSpec as P

TWO_PI = 2.0 * math.pi
ROOT_THREE = math.sqrt(3.0)
MULT = 9
EVEN = (0, 4, 5, 6, 7, 8)
ODD = (1, 2, 3)

SIN_TERMS = (
    4.442883014678955,
    -7.308241367340088,
    3.6062889099121094,
    -0.8457635641098022,
    0.10920575261116028,
)
COS_TERMS = (
    1.4142135381698608,
    -6.978850841522217,
    5.7394609451293945,
    -1.8835630416870117,
    0.31069818139076233,
)


def series(terms, x):
    total = terms[-1]
    for term in terms[-2::-1]:
        total = total * x + term
    return total


def turned(columns, rows):
    turns = columns[0] * rows[0] + columns[1] * rows[1] + columns[2] * rows[2]
    rest = turns - jnp.round(turns)
    square = rest * rest
    half_sin = rest * series(SIN_TERMS, square)
    half_cos = series(COS_TERMS, square)
    cosine = 1.0 - half_sin * half_sin
    sine = half_sin * half_cos
    return cosine.astype(jnp.bfloat16), sine.astype(jnp.bfloat16)


def squared_k(numbers, box_ref):
    parts = [TWO_PI * numbers[x] / box_ref[x] for x in range(3)]
    return parts, parts[0] * parts[0] + parts[1] * parts[1] + parts[2] * parts[2]


def harmonic_rows(numbers, box_ref):
    parts, k_square = squared_k(numbers, box_ref)
    inverse = 1.0 / jnp.sqrt(k_square)
    ux, uy, uz = (part * inverse for part in parts)
    rows = {
        0: None,
        1: ux,
        2: uy,
        3: uz,
        4: -ROOT_THREE * ux * uy,
        5: -ROOT_THREE * uy * uz,
        6: -ROOT_THREE * uz * ux,
        7: -0.5 * ROOT_THREE * (ux * ux - uy * uy),
        8: -0.5 * (3.0 * uz * uz - 1.0),
    }
    return rows, k_square


def times(row, x):
    return x if row is None else row * x


def number_rows(miller_ref, start, width):
    return [
        miller_ref[x : x + 1, pl.ds(start, width)].astype(jnp.float32) for x in range(3)
    ]


def structure_kernel(
    k_block,
    box_ref,
    charges_ref,
    frac_ref,
    counts_ref,
    miller_ref,
    cotangent_ref,
    part_ref,
    phases_ref,
    charges_t,
    columns,
    gain,
    cos_sums,
    sin_sums,
):
    step = pl.program_id(0)
    rows, width = charges_ref.shape
    channels = width // MULT
    k_count = miller_ref.shape[1]
    subs = part_ref.shape[0]
    me = lax.axis_index("dom") * lax.axis_size("sub") + lax.axis_index("sub")

    @pl.when(step == 0)
    def _():
        counts = counts_ref[...]
        lane = lax.broadcasted_iota(jnp.int32, counts.shape, 1)
        mine = jnp.sum(jnp.where(lane == me, counts, 0), axis=1, keepdims=True)
        total = jnp.sum(counts, axis=1, keepdims=True).astype(jnp.float32)
        live = lax.broadcasted_iota(jnp.int32, (rows, 1), 0) < mine
        charges = jnp.where(live, charges_ref[...].astype(jnp.float32), 0.0)
        charges_t[...] = charges.T.astype(jnp.bfloat16)
        coords = frac_ref[...]
        coarse = coords.astype(jnp.bfloat16).astype(jnp.float32)
        fine = (coords - coarse).astype(jnp.bfloat16).astype(jnp.float32)
        position = coarse + fine
        padded = jnp.concatenate([position, jnp.zeros((5, rows), jnp.float32)], axis=0)
        columns[...] = padded.T
        all_numbers = number_rows(miller_ref, 0, k_count)
        _, all_square = squared_k(all_numbers, box_ref)
        all_filter = jnp.exp(-0.5 * all_square) / all_square
        norm = jnp.sqrt(jnp.sum(all_filter * all_filter, axis=1, keepdims=True))
        cotangent = jnp.broadcast_to(cotangent_ref[...], (8, channels)).T[:, 0:1]
        gain[...] = cotangent / (norm * jnp.sqrt(total))

    start = pl.multiple_of(step * k_block, k_block)
    numbers = number_rows(miller_ref, start, k_block)
    table, k_square = harmonic_rows(numbers, box_ref)
    k_filter = jnp.exp(-0.5 * k_square) / k_square
    position = [columns[:, x : x + 1] for x in range(3)]
    cosine, sine = turned(position, numbers)
    phases_ref[0, 0] = cosine
    phases_ref[0, 1] = sine
    cos_sums[...] = jnp.dot(charges_t[...], cosine, preferred_element_type=jnp.float32)
    sin_sums[...] = jnp.dot(charges_t[...], sine, preferred_element_type=jnp.float32)
    share = channels // subs
    for s in range(subs):
        real_part = imag_part = None
        for m in range(MULT):
            at = pl.ds(m * channels + s * share, share)
            with_cos = times(table[m], cos_sums[at, :])
            with_sin = times(table[m], sin_sums[at, :])
            if m in ODD:
                with_cos, with_sin = -with_sin, with_cos
            real_part = with_cos if real_part is None else real_part + with_cos
            imag_part = with_sin if imag_part is None else imag_part + with_sin
        scale = gain[s * share : (s + 1) * share, :] * k_filter
        part_ref[s, 0, 0] = (real_part * scale).astype(jnp.bfloat16)
        part_ref[s, 0, 1] = (imag_part * scale).astype(jnp.bfloat16)


def gradient_kernel(
    k_block,
    box_ref,
    charges_ref,
    counts_ref,
    miller_ref,
    factor_ref,
    phases_ref,
    grad_q_ref,
    grad_f_ref,
    cos_coef,
    sin_coef,
    turned_by,
):
    step = pl.program_id(0)
    rows, width = charges_ref.shape
    channels = width // MULT
    subs = factor_ref.shape[0]
    me = lax.axis_index("dom") * lax.axis_size("sub") + lax.axis_index("sub")

    @pl.when(step == 0)
    def _():
        grad_q_ref[...] = jnp.zeros_like(grad_q_ref)
        turned_by[...] = jnp.zeros_like(turned_by)

    start = pl.multiple_of(step * k_block, k_block)
    numbers = number_rows(miller_ref, start, k_block)
    table, _ = harmonic_rows(numbers, box_ref)
    share = channels // subs
    for s in range(subs):
        real = factor_ref[s, 0, 0].astype(jnp.float32)
        imag = factor_ref[s, 0, 1].astype(jnp.float32)
        for m in range(MULT):
            at = pl.ds(m * channels + s * share, share)
            first, second = (imag, -real) if m in ODD else (real, imag)
            cos_coef[at, :] = times(table[m], first).astype(jnp.bfloat16)
            sin_coef[at, :] = times(table[m], second).astype(jnp.bfloat16)
    charges = charges_ref[...]
    with_sin = jnp.dot(charges, sin_coef[...], preferred_element_type=jnp.float32)
    with_cos = jnp.dot(charges, cos_coef[...], preferred_element_type=jnp.float32)
    cosine = phases_ref[0, 0]
    sine = phases_ref[0, 1]
    turning = cosine.astype(jnp.float32) * with_sin - sine.astype(jnp.float32) * with_cos
    for x in range(3):
        moved = turning * numbers[x]
        folded = moved[:, 0:128]
        for at in range(128, k_block, 128):
            folded = folded + moved[:, at : at + 128]
        turned_by[x] += folded
    contract = (((1,), (1,)), ((), ()))
    grad_q_ref[...] += lax.dot_general(
        cosine, cos_coef[...], contract, preferred_element_type=jnp.float32
    ) + lax.dot_general(sine, sin_coef[...], contract, preferred_element_type=jnp.float32)

    @pl.when(step == pl.num_programs(0) - 1)
    def _():
        counts = counts_ref[...]
        lane = lax.broadcasted_iota(jnp.int32, counts.shape, 1)
        mine = jnp.sum(jnp.where(lane == me, counts, 0), axis=1, keepdims=True)
        live = lax.broadcasted_iota(jnp.int32, (rows, 1), 0) < mine
        grad_q_ref[...] = jnp.where(live, grad_q_ref[...], 0.0)
        live_lane = lax.broadcasted_iota(jnp.int32, (1, rows), 1) < mine
        for x in range(3):
            moved = TWO_PI * jnp.sum(turned_by[x].T, axis=0, keepdims=True)
            grad_f_ref[x : x + 1, :] = jnp.where(live_lane, moved, 0.0)


def whole(shape):
    return pl.BlockSpec(shape, lambda j: (0,) * len(shape))


SMEM = pl.BlockSpec(memory_space=pltpu.SMEM)


def local(charges, frac_coords, atom_counts, miller, box, cotangent):
    doms = lax.axis_size("dom")
    subs = lax.axis_size("sub")
    rows, width = charges.shape
    channels = width // MULT
    k_count = miller.shape[1]
    k_block = k_count // doms
    share = channels // subs
    counts = atom_counts[None, :]
    part, phases = pl.pallas_call(
        functools.partial(structure_kernel, k_block),
        grid=(doms,),
        in_specs=[
            SMEM,
            whole((rows, width)),
            whole((3, rows)),
            whole((1, doms * subs)),
            whole((3, k_count)),
            whole((1, channels)),
        ],
        out_specs=[
            pl.BlockSpec((subs, 1, 2, share, k_block), lambda j: (0, j, 0, 0, 0)),
            pl.BlockSpec((1, 2, rows, k_block), lambda j: (j, 0, 0, 0)),
        ],
        out_shape=[
            jax.ShapeDtypeStruct((subs, doms, 2, share, k_block), jnp.bfloat16),
            jax.ShapeDtypeStruct((doms, 2, rows, k_block), jnp.bfloat16),
        ],
        scratch_shapes=[
            pltpu.VMEM((width, rows), jnp.bfloat16),
            pltpu.VMEM((rows, 8), jnp.float32),
            pltpu.VMEM((channels, 1), jnp.float32),
            pltpu.VMEM((width, k_block), jnp.float32),
            pltpu.VMEM((width, k_block), jnp.float32),
        ],
        name="structure",
    )(box, charges, frac_coords, counts, miller, cotangent[None, :])
    arrived = lax.all_to_all(part, "sub", 0, 0, tiled=True)
    over_sub = jnp.sum(arrived.astype(jnp.float32), axis=0).astype(jnp.bfloat16)
    arrived = lax.all_to_all(over_sub, "dom", 0, 0, tiled=True)
    factor = jnp.sum(arrived.astype(jnp.float32), axis=0).astype(jnp.bfloat16)
    factor = lax.all_gather(factor, "dom", axis=0, tiled=False)
    factor = lax.all_gather(factor, "sub", axis=0, tiled=False)
    grad_q, grad_f = pl.pallas_call(
        functools.partial(gradient_kernel, k_block),
        grid=(doms,),
        in_specs=[
            SMEM,
            whole((rows, width)),
            whole((1, doms * subs)),
            whole((3, k_count)),
            pl.BlockSpec((subs, 1, 2, share, k_block), lambda j: (0, j, 0, 0, 0)),
            pl.BlockSpec((1, 2, rows, k_block), lambda j: (j, 0, 0, 0)),
        ],
        out_specs=[whole((rows, width)), whole((3, rows))],
        out_shape=[
            jax.ShapeDtypeStruct((rows, width), jnp.float32),
            jax.ShapeDtypeStruct((3, rows), jnp.float32),
        ],
        scratch_shapes=[
            pltpu.VMEM((width, k_block), jnp.bfloat16),
            pltpu.VMEM((width, k_block), jnp.bfloat16),
            pltpu.VMEM((3, rows, 128), jnp.float32),
        ],
        name="gradient",
    )(box, charges, counts, miller, factor, phases)
    return grad_q, grad_f


def solution(mesh):
    in_specs = (P(("dom", "sub"), None), P(None, ("dom", "sub")), P(), P(), P(), P())
    out_specs = (P(("dom", "sub"), None), P(None, ("dom", "sub")))
    return jax.shard_map(local, mesh=mesh, in_specs=in_specs, out_specs=out_specs, check_vma=False)
```

```python
import functools
import math

import jax
import jax.numpy as jnp
from jax import lax
from jax.experimental import pallas as pl
from jax.experimental.pallas import tpu as pltpu
from jax.sharding import PartitionSpec as P

TWO_PI = 2.0 * math.pi
ROOT_THREE = math.sqrt(3.0)
MULT = 9
EVEN = (0, 4, 5, 6, 7, 8)
ODD = (1, 2, 3)

SIN_TERMS = (
    4.442883014678955,
    -7.308241367340088,
    3.6062889099121094,
    -0.8457635641098022,
    0.10920575261116028,
)
COS_TERMS = (
    1.4142135381698608,
    -6.978850841522217,
    5.7394609451293945,
    -1.8835630416870117,
    0.31069818139076233,
)


def series(terms, x):
    total = terms[-1]
    for term in terms[-2::-1]:
        total = total * x + term
    return total


def turned(columns, rows):
    turns = columns[0] * rows[0] + columns[1] * rows[1] + columns[2] * rows[2]
    rest = turns - jnp.round(turns)
    square = rest * rest
    half_sin = rest * series(SIN_TERMS, square)
    half_cos = series(COS_TERMS, square)
    cosine = 1.0 - half_sin * half_sin
    sine = half_sin * half_cos
    return cosine.astype(jnp.bfloat16), sine.astype(jnp.bfloat16)


def squared_k(numbers, box_ref):
    parts = [TWO_PI * numbers[x] / box_ref[x] for x in range(3)]
    return parts, parts[0] * parts[0] + parts[1] * parts[1] + parts[2] * parts[2]


def harmonic_rows(numbers, box_ref):
    parts, k_square = squared_k(numbers, box_ref)
    inverse = 1.0 / jnp.sqrt(k_square)
    ux, uy, uz = (part * inverse for part in parts)
    rows = {
        0: None,
        1: ux,
        2: uy,
        3: uz,
        4: -ROOT_THREE * ux * uy,
        5: -ROOT_THREE * uy * uz,
        6: -ROOT_THREE * uz * ux,
        7: -0.5 * ROOT_THREE * (ux * ux - uy * uy),
        8: -0.5 * (3.0 * uz * uz - 1.0),
    }
    return rows, k_square


def times(row, x):
    return x if row is None else row * x


def number_rows(miller_ref, start, width):
    return [
        miller_ref[x : x + 1, pl.ds(start, width)].astype(jnp.float32) for x in range(3)
    ]


def live_rows(counts, me, shape, dim):
    lane = lax.broadcasted_iota(jnp.int32, counts.shape, 1)
    mine = jnp.sum(jnp.where(lane == me, counts, 0), axis=1, keepdims=True)
    return lax.broadcasted_iota(jnp.int32, shape, dim) < mine


def my_device():
    return lax.axis_index("dom") * lax.axis_size("sub") + lax.axis_index("sub")


def my_core():
    return lax.rem(lax.axis_index("sub"), 2)


def structure_kernel(
    k_block,
    box_ref,
    charges_ref,
    frac_ref,
    counts_ref,
    miller_ref,
    cotangent_ref,
    mine_ref,
    theirs_ref,
    phases_ref,
    charges_t,
    columns,
    gain,
    phases_0,
    phases_1,
    sums_0,
    sums_1,
):
    step = pl.program_id(0)
    rows, width = charges_ref.shape
    channels = width // MULT
    half = channels // 2
    k_count = miller_ref.shape[1]
    core = my_core()

    def block_numbers(block):
        start = pl.multiple_of(jnp.minimum(block * k_block, k_count - k_block), k_block)
        return number_rows(miller_ref, start, k_block)

    def write_phases(block, to):
        position = [columns[:, x : x + 1] for x in range(3)]
        cosine, sine = turned(position, block_numbers(block))
        to[0] = cosine
        to[1] = sine

    @pl.when(step == 0)
    def _():
        counts = counts_ref[...]
        total = jnp.sum(counts, axis=1, keepdims=True).astype(jnp.float32)
        live = live_rows(counts, my_device(), (rows, 1), 0)
        charges = jnp.where(live, charges_ref[...].astype(jnp.float32), 0.0)
        charges_t[...] = charges.T.astype(jnp.bfloat16)
        coords = frac_ref[...]
        coarse = coords.astype(jnp.bfloat16).astype(jnp.float32)
        fine = (coords - coarse).astype(jnp.bfloat16).astype(jnp.float32)
        position = coarse + fine
        padded = jnp.concatenate([position, jnp.zeros((5, rows), jnp.float32)], axis=0)
        columns[...] = padded.T
        all_numbers = number_rows(miller_ref, 0, k_count)
        _, all_square = squared_k(all_numbers, box_ref)
        all_filter = jnp.exp(-0.5 * all_square) / all_square
        norm = jnp.sqrt(jnp.sum(all_filter * all_filter, axis=1, keepdims=True))
        cotangent = jnp.broadcast_to(cotangent_ref[...], (8, channels)).T[:, 0:1]
        gain[...] = cotangent / (norm * jnp.sqrt(total))
        write_phases(0, phases_0)

    def one_block(part, phases, sums, following, other):
        block = 2 * step + part
        table, k_square = harmonic_rows(block_numbers(block), box_ref)
        k_filter = jnp.exp(-0.5 * k_square) / k_square
        sums[0] = jnp.dot(charges_t[...], phases[0], preferred_element_type=jnp.float32)
        sums[1] = jnp.dot(charges_t[...], phases[1], preferred_element_type=jnp.float32)
        phases_ref[part, 0] = phases[0]
        phases_ref[part, 1] = phases[1]
        write_phases(following, other)
        for ref, owner in ((mine_ref, core), (theirs_ref, 1 - core)):
            for at in range(0, half, 16):
                real_part = imag_part = None
                for m in range(MULT):
                    start = pl.multiple_of(m * channels + owner * half + at, 16)
                    with_cos = times(table[m], sums[0, pl.ds(start, 16), :])
                    with_sin = times(table[m], sums[1, pl.ds(start, 16), :])
                    if m in ODD:
                        with_cos, with_sin = -with_sin, with_cos
                    real_part = with_cos if real_part is None else real_part + with_cos
                    imag_part = with_sin if imag_part is None else imag_part + with_sin
                scale = gain[pl.ds(pl.multiple_of(owner * half + at, 16), 16), :] * k_filter
                ref[part, 0, at : at + 16] = (real_part * scale).astype(ref.dtype)
                ref[part, 1, at : at + 16] = (imag_part * scale).astype(ref.dtype)

    one_block(0, phases_0, sums_0, 2 * step + 1, phases_1)
    one_block(1, phases_1, sums_1, 2 * step + 2, phases_0)


def gradient_kernel(
    k_block,
    box_ref,
    charges_ref,
    counts_ref,
    miller_ref,
    mine_ref,
    theirs_ref,
    phases_ref,
    grad_q_ref,
    grad_f_ref,
    cos_coef,
    sin_coef,
    turned_by,
):
    step = pl.program_id(0)
    rows, width = charges_ref.shape
    channels = width // MULT
    half = channels // 2
    core = my_core()

    @pl.when(step == 0)
    def _():
        grad_q_ref[...] = jnp.zeros_like(grad_q_ref)
        turned_by[...] = jnp.zeros_like(turned_by)

    start = pl.multiple_of(step * k_block, k_block)
    numbers = number_rows(miller_ref, start, k_block)
    table, _ = harmonic_rows(numbers, box_ref)
    for ref, owner in ((mine_ref, core), (theirs_ref, 1 - core)):
        for at in range(0, half, 16):
            real = ref[0, 0, at : at + 16].astype(jnp.float32)
            imag = ref[0, 1, at : at + 16].astype(jnp.float32)
            for m in range(MULT):
                start = pl.multiple_of(m * channels + owner * half + at, 16)
                first, second = (imag, -real) if m in ODD else (real, imag)
                cos_coef[pl.ds(start, 16), :] = times(table[m], first).astype(jnp.bfloat16)
                sin_coef[pl.ds(start, 16), :] = times(table[m], second).astype(jnp.bfloat16)
    charges = charges_ref[...]
    with_sin = jnp.dot(charges, sin_coef[...], preferred_element_type=jnp.float32)
    with_cos = jnp.dot(charges, cos_coef[...], preferred_element_type=jnp.float32)
    cosine = phases_ref[0, 0]
    sine = phases_ref[0, 1]
    turning = cosine.astype(jnp.float32) * with_sin - sine.astype(jnp.float32) * with_cos
    for x in range(3):
        moved = turning * numbers[x]
        folded = moved[:, 0:128]
        for at in range(128, k_block, 128):
            folded = folded + moved[:, at : at + 128]
        turned_by[x] += folded
    contract = (((1,), (1,)), ((), ()))
    grad_q_ref[...] += lax.dot_general(
        cosine, cos_coef[...], contract, preferred_element_type=jnp.float32
    ) + lax.dot_general(sine, sin_coef[...], contract, preferred_element_type=jnp.float32)

    @pl.when(step == pl.num_programs(0) - 1)
    def _():
        live = live_rows(counts_ref[...], my_device(), (rows, 1), 0)
        grad_q_ref[...] = jnp.where(live, grad_q_ref[...], 0.0)
        live_lane = live_rows(counts_ref[...], my_device(), (1, rows), 1)
        for x in range(3):
            moved = TWO_PI * jnp.sum(turned_by[x].T, axis=0, keepdims=True)
            grad_f_ref[x : x + 1, :] = jnp.where(live_lane, moved, 0.0)


def whole(shape):
    return pl.BlockSpec(shape, lambda j: (0,) * len(shape))


SMEM = pl.BlockSpec(memory_space=pltpu.SMEM)


def neighbours(doms, subs, moved):
    return [
        (dom * subs + sub, dom * subs + moved(sub)) for dom in range(doms) for sub in range(subs)
    ]


def local(charges, frac_coords, atom_counts, miller, box, cotangent):
    axes = ("dom", "sub")
    doms = lax.axis_size("dom")
    subs = lax.axis_size("sub")
    rows, width = charges.shape
    channels = width // MULT
    half = channels // 2
    k_count = miller.shape[1]
    k_block = k_count // doms
    counts = atom_counts[None, :]
    share = (doms, 2, half, k_block)
    share_pair = pl.BlockSpec((2, 2, half, k_block), lambda j: (j, 0, 0, 0))
    mine, theirs, phases = pl.pallas_call(
        functools.partial(structure_kernel, k_block),
        grid=(doms // 2,),
        in_specs=[
            SMEM,
            whole((rows, width)),
            whole((3, rows)),
            whole((1, doms * subs)),
            whole((3, k_count)),
            whole((1, channels)),
        ],
        out_specs=[
            share_pair,
            share_pair,
            pl.BlockSpec((2, 2, rows, k_block), lambda j: (j, 0, 0, 0)),
        ],
        out_shape=[
            jax.ShapeDtypeStruct(share, jnp.float32),
            jax.ShapeDtypeStruct(share, jnp.bfloat16),
            jax.ShapeDtypeStruct((doms, 2, rows, k_block), jnp.bfloat16),
        ],
        scratch_shapes=[
            pltpu.VMEM((width, rows), jnp.bfloat16),
            pltpu.VMEM((rows, 8), jnp.float32),
            pltpu.VMEM((channels, 1), jnp.float32),
            pltpu.VMEM((2, rows, k_block), jnp.bfloat16),
            pltpu.VMEM((2, rows, k_block), jnp.bfloat16),
            pltpu.VMEM((2, width, k_block), jnp.float32),
            pltpu.VMEM((2, width, k_block), jnp.float32),
        ],
        name="structure",
    )(box, charges, frac_coords, counts, miller, cotangent[None, :])
    other_core = neighbours(doms, subs, lambda sub: sub ^ 1)
    along_x = [
        neighbours(doms, subs, lambda sub, by=by: (sub + by) % subs) for by in range(2, subs, 2)
    ]
    arrived = lax.ppermute(theirs, axes, other_core)
    on_chip = (mine + arrived.astype(jnp.float32)).astype(jnp.bfloat16)
    arrived = lax.all_to_all(on_chip, "dom", 0, 0, tiled=True)
    summed = jnp.sum(arrived.astype(jnp.float32), axis=0)
    sent = summed.astype(jnp.bfloat16)
    for pairs in along_x:
        summed = summed + lax.ppermute(sent, axes, pairs).astype(jnp.float32)
    factor = summed.astype(jnp.bfloat16)
    mine = lax.all_to_all(jnp.broadcast_to(factor[None], share), "dom", 0, 0, tiled=True)
    theirs = lax.ppermute(mine, axes, other_core)
    share_one = pl.BlockSpec((1, 2, half, k_block), lambda j: (j, 0, 0, 0))
    grad_q, grad_f = pl.pallas_call(
        functools.partial(gradient_kernel, k_block),
        grid=(doms,),
        in_specs=[
            SMEM,
            whole((rows, width)),
            whole((1, doms * subs)),
            whole((3, k_count)),
            share_one,
            share_one,
            pl.BlockSpec((1, 2, rows, k_block), lambda j: (j, 0, 0, 0)),
        ],
        out_specs=[whole((rows, width)), whole((3, rows))],
        out_shape=[
            jax.ShapeDtypeStruct((rows, width), jnp.float32),
            jax.ShapeDtypeStruct((3, rows), jnp.float32),
        ],
        scratch_shapes=[
            pltpu.VMEM((width, k_block), jnp.bfloat16),
            pltpu.VMEM((width, k_block), jnp.bfloat16),
            pltpu.VMEM((3, rows, 128), jnp.float32),
        ],
        name="gradient",
    )(box, charges, counts, miller, mine, theirs, phases)
    return grad_q, grad_f


def solution(mesh):
    in_specs = (P(("dom", "sub"), None), P(None, ("dom", "sub")), P(), P(), P(), P())
    out_specs = (P(("dom", "sub"), None), P(None, ("dom", "sub")))
    return jax.shard_map(local, mesh=mesh, in_specs=in_specs, out_specs=out_specs, check_vma=False)
```

```python
import functools
import math

import jax
import jax.numpy as jnp
from jax import lax
from jax.experimental import pallas as pl
from jax.experimental.pallas import tpu as pltpu
from jax.sharding import PartitionSpec as P

TWO_PI = 2.0 * math.pi
ROOT_THREE = math.sqrt(3.0)
MULT = 9
ODD = (1, 2, 3)
VMEM_LIMIT = 24 * 2**20
PHASE_ROWS = 32
TURNED_ROWS = 32
WITH_CHUNKS = 1
LEAD = 0.5
SUM_CHUNKS = 4

SIN_TERMS = (
    4.442883014678955,
    -7.308241367340088,
    3.6062889099121094,
    -0.8457635641098022,
    0.10920575261116028,
)
COS_TERMS = (
    1.4142135381698608,
    -6.978850841522217,
    5.7394609451293945,
    -1.8835630416870117,
    0.31069818139076233,
)


def series(terms, x):
    total = terms[-1]
    for term in terms[-2::-1]:
        total = total * x + term
    return total


def turned(turns):
    rest = turns - jnp.round(turns)
    square = rest * rest
    half_sin = rest * series(SIN_TERMS, square)
    half_cos = series(COS_TERMS, square)
    cosine = 1.0 - half_sin * half_sin
    sine = half_sin * half_cos
    return cosine.astype(jnp.bfloat16), sine.astype(jnp.bfloat16)


def squared_k(numbers, box_ref):
    parts = [TWO_PI * numbers[x] / box_ref[x] for x in range(3)]
    return parts, parts[0] * parts[0] + parts[1] * parts[1] + parts[2] * parts[2]


def harmonic_rows(numbers, box_ref):
    parts, k_square = squared_k(numbers, box_ref)
    inverse = 1.0 / jnp.sqrt(k_square)
    ux, uy, uz = (part * inverse for part in parts)
    rows = {
        0: None,
        1: ux,
        2: uy,
        3: uz,
        4: -ROOT_THREE * ux * uy,
        5: -ROOT_THREE * uy * uz,
        6: -ROOT_THREE * uz * ux,
        7: -0.5 * ROOT_THREE * (ux * ux - uy * uy),
        8: -0.5 * (3.0 * uz * uz - 1.0),
    }
    return rows, k_square


def times(row, x):
    return x if row is None else row * x


def number_rows(miller_ref, start, width):
    return [
        miller_ref[x : x + 1, pl.ds(start, width)].astype(jnp.float32) for x in range(3)
    ]


def run_together(*writers):
    placed = []
    for order, pieces in enumerate(writers):
        whole_cost = sum(cost for cost, _ in pieces)
        done = 0.0
        for cost, piece in pieces:
            placed.append(((done + LEAD * cost) / whole_cost, order, len(placed), piece))
            done += cost
    for entry in sorted(placed, key=lambda entry: entry[:3]):
        entry[3]()


def live_rows(counts, me, shape, dim):
    lane = lax.broadcasted_iota(jnp.int32, counts.shape, 1)
    mine = jnp.sum(jnp.where(lane == me, counts, 0), axis=1, keepdims=True)
    return lax.broadcasted_iota(jnp.int32, shape, dim) < mine


def my_device():
    return lax.axis_index("dom") * lax.axis_size("sub") + lax.axis_index("sub")


def my_core():
    return lax.rem(lax.axis_index("sub"), 2)


def structure_kernel(
    k_block,
    box_ref,
    charges_ref,
    frac_ref,
    counts_ref,
    miller_ref,
    cotangent_ref,
    mine_ref,
    theirs_ref,
    phases_ref,
    charges_t,
    columns,
    gain,
    turns_0,
    turns_1,
    phases_0,
    phases_1,
    sums_0,
    sums_1,
    table_0,
    table_1,
):
    step = pl.program_id(0)
    rows, width = charges_ref.shape
    channels = width // MULT
    half = channels // 2
    k_count = miller_ref.shape[1]
    lanes = k_block // 128
    core = my_core()

    def block_numbers(block):
        start = pl.multiple_of(jnp.clip(block * k_block, 0, k_count - k_block), k_block)
        return number_rows(miller_ref, start, k_block)

    def write_turns(block, turns):
        numbers = block_numbers(block)
        blank = jnp.zeros((10, k_block), jnp.float32)
        both = jnp.concatenate(numbers + numbers + [blank], axis=0).astype(jnp.bfloat16)
        turns[...] = jnp.dot(columns[...], both, preferred_element_type=jnp.float32)

    def write_phases(turns, phases):
        def piece_at(at):
            piece = slice(at, at + PHASE_ROWS)
            cosine, sine = turned(turns[piece, :])
            phases[piece, :k_block] = cosine
            phases[piece, k_block:] = sine

        return [(1, functools.partial(piece_at, at)) for at in range(0, rows, PHASE_ROWS)]

    def write_sums(phases, sums):
        chunk = width // SUM_CHUNKS

        def piece_at(at, kind):
            piece = slice(at, at + chunk)
            sums[kind, piece, :] = jnp.dot(
                charges_t[piece, :],
                phases[:, kind * k_block : (kind + 1) * k_block],
                preferred_element_type=jnp.float32,
            )

        return [
            (1, functools.partial(piece_at, at, kind))
            for at in range(0, width, chunk)
            for kind in range(2)
        ]

    def write_table(block, rows_ref):
        table, k_square = harmonic_rows(block_numbers(block), box_ref)
        rows_ref[0:1, :] = jnp.exp(-0.5 * k_square) / k_square
        for m in range(1, MULT):
            rows_ref[m : m + 1, :] = table[m]

    def write_shares(table, sums):
        def parts_at(at):
            for m in range(MULT):
                with_cos = sums[0, m * channels + at : m * channels + at + 16, :]
                with_sin = sums[1, m * channels + at : m * channels + at + 16, :]
                if m == 0:
                    real, imag = with_cos, with_sin
                    continue
                row = table[m : m + 1, :]
                if m in ODD:
                    real, imag = real - row * with_sin, imag + row * with_cos
                else:
                    real, imag = real + row * with_cos, imag + row * with_sin
            scale = gain[at : at + 16, :] * table[0:1, :]
            return real * scale, imag * scale

        def piece_at(at):
            pairs = zip(parts_at(at), parts_at(half + at))
            for kind, (low, high) in enumerate(pairs):
                mine = jnp.where(core == 0, low, high)
                theirs = jnp.where(core == 0, high, low)
                for lane in range(lanes):
                    first = (kind * lanes + lane) * half + at
                    piece = slice(lane * 128, (lane + 1) * 128)
                    mine_ref[0, first : first + 16, :] = mine[:, piece]
                    theirs_ref[0, first : first + 16, :] = theirs[:, piece].astype(jnp.bfloat16)

        return [(1, functools.partial(piece_at, at)) for at in range(0, half, 16)]

    @pl.when(step == 0)
    def _():
        counts = counts_ref[...]
        total = jnp.sum(counts, axis=1, keepdims=True).astype(jnp.float32)
        live = live_rows(counts, my_device(), (1, rows), 1).astype(jnp.bfloat16)
        charges_t[...] = charges_ref[...].T * live
        coords = frac_ref[...]
        coarse = coords.astype(jnp.bfloat16).astype(jnp.float32)
        fine = (coords - coarse).astype(jnp.bfloat16).astype(jnp.float32)
        padded = jnp.concatenate([coarse, fine, jnp.zeros((10, rows), jnp.float32)], axis=0)
        columns[...] = padded.T.astype(jnp.bfloat16)
        all_numbers = number_rows(miller_ref, 0, k_count)
        _, all_square = squared_k(all_numbers, box_ref)
        all_filter = jnp.exp(-0.5 * all_square) / all_square
        norm = jnp.sqrt(jnp.sum(all_filter * all_filter, axis=1, keepdims=True))
        cotangent = jnp.broadcast_to(cotangent_ref[...], (8, channels)).T[:, 0:1]
        gain[...] = cotangent / (norm * jnp.sqrt(total))
        write_turns(0, turns_0)
        write_turns(1, turns_1)
        run_together(write_phases(turns_0, phases_0))

    turns, phases, sums = (turns_0, turns_1), (phases_0, phases_1), (sums_0, sums_1)
    tables = (table_0, table_1)
    last = pl.num_programs(0) - 1

    for now in range(2):
        other = 1 - now

        @pl.when((step < last) & (lax.rem(step, 2) == now))
        def _(now=now, other=other):
            write_turns(step + 2, turns[now])
            write_table(step, tables[now])
            phases_ref[0] = phases[now][...]
            run_together(
                write_sums(phases[now], sums[now]),
                write_phases(turns[other], phases[other]),
                write_shares(tables[other], sums[other]),
            )

    @pl.when(step == last)
    def _():
        run_together(write_shares(table_1, sums_1))


def gradient_kernel(
    k_block,
    box_ref,
    charges_ref,
    counts_ref,
    miller_ref,
    mine_ref,
    theirs_ref,
    phases_ref,
    before_ref,
    grad_q_ref,
    grad_f_ref,
    turned_by,
    coef_0,
    coef_1,
    with_0,
    with_1,
):
    step = pl.program_id(0)
    last = pl.num_programs(0) - 1
    rows, width = charges_ref.shape
    channels = width // MULT
    half = channels // 2
    k_count = miller_ref.shape[1]
    lanes = k_block // 128
    core = my_core()
    contract = (((1,), (1,)), ((), ()))

    def block_numbers(block):
        start = pl.multiple_of(jnp.clip(block * k_block, 0, k_count - k_block), k_block)
        return number_rows(miller_ref, start, k_block)

    def write_coefs(block, coef):
        table, _ = harmonic_rows(block_numbers(block), box_ref)

        def wide(kind, at):
            low, high = [], []
            for lane in range(lanes):
                first = (kind * lanes + lane) * half + at
                mine = mine_ref[0, first : first + 16, :].astype(jnp.float32)
                theirs = theirs_ref[0, first : first + 16, :].astype(jnp.float32)
                low.append(jnp.where(core == 0, mine, theirs))
                high.append(jnp.where(core == 0, theirs, mine))
            return jnp.concatenate(low, axis=1), jnp.concatenate(high, axis=1)

        def piece_at(at):
            for place, real, imag in zip((at, half + at), wide(0, at), wide(1, at)):
                for m in range(MULT):
                    piece = slice(m * channels + place, m * channels + place + 16)
                    first, second = (imag, -real) if m in ODD else (real, imag)
                    coef[piece, :k_block] = times(table[m], first).astype(jnp.bfloat16)
                    coef[piece, k_block:] = times(table[m], second).astype(jnp.bfloat16)

        return [(1, functools.partial(piece_at, at)) for at in range(0, half, 16)]

    def write_dots(coef, dots):
        part = rows // WITH_CHUNKS

        def with_at(at, kind):
            piece = slice(at, at + part)
            dots[kind, piece, :] = jnp.dot(
                charges_ref[piece, :],
                coef[:, kind * k_block : (kind + 1) * k_block],
                preferred_element_type=jnp.float32,
            )

        def grad_at(at):
            piece = slice(at, min(at + 256, width))
            grad_q_ref[:, piece] += lax.dot_general(
                phases_ref[0], coef[piece, :], contract, preferred_element_type=jnp.float32
            )

        return [
            (5 / WITH_CHUNKS, functools.partial(with_at, at, kind))
            for kind in range(2)
            for at in range(0, rows, part)
        ] + [(2, functools.partial(grad_at, at)) for at in range(0, width, 256)]

    def write_turned(block, dots):
        numbers = block_numbers(block)

        def piece_at(at):
            piece = slice(at, at + TURNED_ROWS)
            cosine = before_ref[0, piece, :k_block].astype(jnp.float32)
            sine = before_ref[0, piece, k_block:].astype(jnp.float32)
            turning = cosine * dots[1, piece, :] - sine * dots[0, piece, :]
            for x in range(3):
                moved = turning * numbers[x]
                folded = moved[:, 0:128]
                for lane in range(1, lanes):
                    folded = folded + moved[:, lane * 128 : (lane + 1) * 128]
                turned_by[x, piece, :] += folded

        return [(1, functools.partial(piece_at, at)) for at in range(0, rows, TURNED_ROWS)]

    coefs, dots = (coef_0, coef_1), (with_0, with_1)

    @pl.when(step == 0)
    def _():
        grad_q_ref[...] = jnp.zeros_like(grad_q_ref)
        turned_by[...] = jnp.zeros_like(turned_by)
        with_1[...] = jnp.zeros_like(with_1)
        run_together(write_coefs(0, coef_0))

    for now in range(2):
        other = 1 - now

        @pl.when((step > 0) & (step < last) & (lax.rem(step, 2) == now))
        def _(now=now, other=other):
            run_together(
                write_dots(coefs[other], dots[other]),
                write_turned(step - 2, dots[now]),
                write_coefs(step, coefs[now]),
            )

    @pl.when(step == last)
    def _():
        run_together(write_turned(step - 2, with_1))
        live = live_rows(counts_ref[...], my_device(), (rows, 1), 0)
        grad_q_ref[...] = jnp.where(live, grad_q_ref[...], 0.0)
        live_lane = live_rows(counts_ref[...], my_device(), (1, rows), 1)
        for x in range(3):
            moved = TWO_PI * jnp.sum(turned_by[x].T, axis=0, keepdims=True)
            grad_f_ref[x : x + 1, :] = jnp.where(live_lane, moved, 0.0)


def whole(shape):
    return pl.BlockSpec(shape, lambda j: (0,) * len(shape))


SMEM = pl.BlockSpec(memory_space=pltpu.SMEM)


def neighbours(doms, subs, moved):
    return [
        (dom * subs + sub, dom * subs + moved(sub)) for dom in range(doms) for sub in range(subs)
    ]


def local(charges, frac_coords, atom_counts, miller, box, cotangent):
    axes = ("dom", "sub")
    doms = lax.axis_size("dom")
    subs = lax.axis_size("sub")
    rows, width = charges.shape
    channels = width // MULT
    half = channels // 2
    k_count = miller.shape[1]
    k_block = k_count // doms
    counts = atom_counts[None, :]
    lines = 2 * half * k_block // 128
    share = (doms, lines, 128)
    share_late = pl.BlockSpec((1, lines, 128), lambda j: (jnp.maximum(j - 1, 0), 0, 0))
    mine, theirs, phases = pl.pallas_call(
        functools.partial(structure_kernel, k_block),
        grid=(doms + 1,),
        in_specs=[
            SMEM,
            whole((rows, width)),
            whole((3, rows)),
            whole((1, doms * subs)),
            whole((3, k_count)),
            whole((1, channels)),
        ],
        out_specs=[
            share_late,
            share_late,
            pl.BlockSpec((1, rows, 2 * k_block), lambda j: (jnp.minimum(j, doms - 1), 0, 0)),
        ],
        out_shape=[
            jax.ShapeDtypeStruct(share, jnp.float32),
            jax.ShapeDtypeStruct(share, jnp.bfloat16),
            jax.ShapeDtypeStruct((doms, rows, 2 * k_block), jnp.bfloat16),
        ],
        scratch_shapes=[
            pltpu.VMEM((width, rows), jnp.bfloat16),
            pltpu.VMEM((rows, 16), jnp.bfloat16),
            pltpu.VMEM((channels, 1), jnp.float32),
            pltpu.VMEM((rows, k_block), jnp.float32),
            pltpu.VMEM((rows, k_block), jnp.float32),
            pltpu.VMEM((rows, 2 * k_block), jnp.bfloat16),
            pltpu.VMEM((rows, 2 * k_block), jnp.bfloat16),
            pltpu.VMEM((2, width, k_block), jnp.float32),
            pltpu.VMEM((2, width, k_block), jnp.float32),
            pltpu.VMEM((16, k_block), jnp.float32),
            pltpu.VMEM((16, k_block), jnp.float32),
        ],
        compiler_params=pltpu.CompilerParams(vmem_limit_bytes=VMEM_LIMIT),
        name="structure",
    )(box, charges, frac_coords, counts, miller, cotangent[None, :])
    other_core = neighbours(doms, subs, lambda sub: sub ^ 1)
    along_x = [
        neighbours(doms, subs, lambda sub, by=by: (sub + by) % subs) for by in range(2, subs, 2)
    ]
    arrived = lax.ppermute(theirs, axes, other_core)
    on_chip = (mine + arrived.astype(jnp.float32)).astype(jnp.bfloat16)
    arrived = lax.all_to_all(on_chip, "dom", 0, 0, tiled=True)
    summed = jnp.sum(arrived.astype(jnp.float32), axis=0)
    sent = summed.astype(jnp.bfloat16)
    for pairs in along_x:
        summed = summed + lax.ppermute(sent, axes, pairs).astype(jnp.float32)
    factor = summed.astype(jnp.bfloat16)
    mine = lax.all_to_all(jnp.broadcast_to(factor[None], share), "dom", 0, 0, tiled=True)
    theirs = lax.ppermute(mine, axes, other_core)
    share_next = pl.BlockSpec((1, lines, 128), lambda j: (jnp.minimum(j, doms - 1), 0, 0))
    grad_q, grad_f = pl.pallas_call(
        functools.partial(gradient_kernel, k_block),
        grid=(doms + 2,),
        in_specs=[
            SMEM,
            whole((rows, width)),
            whole((1, doms * subs)),
            whole((3, k_count)),
            share_next,
            share_next,
            pl.BlockSpec((1, rows, 2 * k_block), lambda j: (jnp.clip(j - 1, 0, doms - 1), 0, 0)),
            pl.BlockSpec((1, rows, 2 * k_block), lambda j: (jnp.clip(j - 2, 0, doms - 1), 0, 0)),
        ],
        out_specs=[whole((rows, width)), whole((3, rows))],
        out_shape=[
            jax.ShapeDtypeStruct((rows, width), jnp.float32),
            jax.ShapeDtypeStruct((3, rows), jnp.float32),
        ],
        scratch_shapes=[
            pltpu.VMEM((3, rows, 128), jnp.float32),
            pltpu.VMEM((width, 2 * k_block), jnp.bfloat16),
            pltpu.VMEM((width, 2 * k_block), jnp.bfloat16),
            pltpu.VMEM((2, rows, k_block), jnp.float32),
            pltpu.VMEM((2, rows, k_block), jnp.float32),
        ],
        compiler_params=pltpu.CompilerParams(vmem_limit_bytes=VMEM_LIMIT),
        name="gradient",
    )(box, charges, counts, miller, mine, theirs, phases, phases)
    return grad_q, grad_f


def solution(mesh):
    in_specs = (P(("dom", "sub"), None), P(None, ("dom", "sub")), P(), P(), P(), P())
    out_specs = (P(("dom", "sub"), None), P(None, ("dom", "sub")))
    return jax.shard_map(local, mesh=mesh, in_specs=in_specs, out_specs=out_specs, check_vma=False)
```
